256 devices in a mesh: seq: 256 (over z, y, x, core).
Axes of the slice: x: 4, y: 4, z: 8, core: 2. Of those that a mesh axis runs over, the one named last changes fastest.
Arguments:
- tokens: bfloat16 [65536, 768], P('seq'), may hold values from -64 to 64
- w_query: bfloat16 [768, 768], replicated, may hold values from -0.21875 to 0.21875
- w_key: bfloat16 [768, 768], replicated, may hold values from -0.21875 to 0.21875
- w_value: bfloat16 [768, 768], replicated, may hold values from -0.21875 to 0.21875
- w_out: bfloat16 [768, 768], replicated, may hold values from -0.21875 to 0.21875
- ln_gain: float32 [768], replicated, may hold values from 0.5 to 1.5
- ln_bias: float32 [768], replicated, may hold values from -3 to 3
Outputs:
- encoded: bfloat16 [65536, 768], P('seq')
The draws below stay inside these ranges and needn't reach their ends.
All inputs are finite; a program needn't handle non-finite values.
Results may differ from the reference program's by a relative error of at most 0.003.
The reference program's roundings to bfloat16 on the way count: a program that leaves them out, or rounds other values in their place, can miss the bound.
Values may be sent and summed in bfloat16 or wider, within the bound.
No kernel may reach another device: no remote copies, remote signals or barrier semaphores. Data moves between devices by JAX's collectives and lax.ppermute only.
A program may use at most 256 MiB of HBM per device.

```python
import math
import jax
import jax.numpy as jnp
from jax import lax

D = 768
H = 12
BLOCK = 64
NG = 128
TOK_DEV = 256
TOKENS = 65536


def draw_tokens(key, part):
    first_key = jax.random.fold_in(key, 101)
    third_key = jax.random.fold_in(key, 303)
    fourth_key = jax.random.fold_in(key, 404)
    fifth_key = jax.random.fold_in(key, 505)
    base_rows = jnp.clip(jax.random.normal(first_key, (TOKENS, D), jnp.float32), -4.0, 4.0)
    shards = TOKENS // TOK_DEV
    global_scale = 1.0
    low_strength = 10.0
    high_strength = 14.0
    row_ids = jnp.arange(TOKENS, dtype=jnp.int32)
    base_rows = base_rows * jnp.where(row_ids < NG, global_scale, 1.0)[:, None]
    device_ids = jnp.arange(shards, dtype=jnp.int32)
    targets = device_ids // 2 % NG
    places = device_ids * TOK_DEV + TOK_DEV - 1
    pair_draw = jax.random.uniform(third_key, (shards,), jnp.float32, low_strength, high_strength)
    strength = pair_draw[device_ids // 2]
    shrink = 1.0 - jnp.where(device_ids % 2 == 1, jax.random.uniform(fourth_key, (shards,), jnp.float32, 0.02, 0.08), 0.0)
    fresh_rows = jnp.clip(jax.random.normal(fifth_key, (shards, D), jnp.float32), -4.0, 4.0)
    aligned = (strength * shrink)[:, None] * base_rows[targets] + fresh_rows
    result_rows = base_rows.at[places].set(aligned)
    return jnp.clip(result_rows, -64.0, 64.0).astype(jnp.bfloat16)


def scatter_about(key, extent, scale, reach, kind=jnp.bfloat16):
    return jnp.clip(scale * jax.random.normal(key, extent, jnp.float32), -reach, reach).astype(kind)


def setup_inputs(seed: int = 0) -> dict:
    splits = jax.random.split(jax.random.key(seed), 8)
    tokens = draw_tokens(jax.random.fold_in(splits[7], 71), 0)
    w_query = scatter_about(splits[1], (D, D), D ** -0.5, 0.21875)
    w_key = scatter_about(splits[2], (D, D), D ** -0.5, 0.21875)
    w_value = scatter_about(splits[3], (D, D), D ** -0.5, 0.21875)
    w_out = scatter_about(splits[4], (D, D), D ** -0.5, 0.21875)
    ln_gain = jnp.clip(1.0 + 0.1 * jax.random.normal(splits[5], (D,), jnp.float32), 0.5, 1.5)
    ln_bias = scatter_about(splits[6], (D,), 0.5, 3.0, jnp.float32)
    return dict(tokens=tokens, w_query=w_query, w_key=w_key, w_value=w_value, w_out=w_out, ln_gain=ln_gain, ln_bias=ln_bias)


def layer_norm(summed, ln_gain, ln_bias):
    center = summed - lax.optimization_barrier(jnp.mean(summed, axis=-1, keepdims=True))
    spread = lax.optimization_barrier(jnp.mean(center * center, axis=-1, keepdims=True))
    return center * lax.rsqrt(spread + 1e-05) * ln_gain + ln_bias

def reference(tokens, w_query, w_key, w_value, w_out, ln_gain, ln_bias):
    head_dim = D // H
    factor = 1.0 / math.sqrt(head_dim)
    query_rows = jnp.dot(tokens, w_query, preferred_element_type=jnp.float32).astype(jnp.bfloat16)
    key_rows = jnp.dot(tokens, w_key, preferred_element_type=jnp.float32).astype(jnp.bfloat16)
    value_rows = jnp.dot(tokens, w_value, preferred_element_type=jnp.float32).astype(jnp.bfloat16)
    blocks = TOKENS // BLOCK
    group_size = math.gcd(blocks, 16)
    query_blocks = query_rows.reshape(blocks, BLOCK, H, head_dim)
    pad_spec = ((1, 1), (0, 0), (0, 0), (0, 0))
    key_padded = jnp.pad(key_rows.reshape(blocks, BLOCK, H, head_dim), pad_spec)
    value_padded = jnp.pad(value_rows.reshape(blocks, BLOCK, H, head_dim), pad_spec)
    global_keys = key_rows[:NG].reshape(NG, H, head_dim).astype(jnp.float32)
    global_values = value_rows[:NG].reshape(NG, H, head_dim).astype(jnp.float32)
    offsets = jnp.arange(3 * BLOCK, dtype=jnp.int32)

    def window_group(group_index):
        first_block = group_index * group_size
        query_part = lax.dynamic_slice_in_dim(query_blocks, first_block, group_size, 0).astype(jnp.float32)
        key_part = lax.dynamic_slice_in_dim(key_padded, first_block, group_size + 2, 0)
        value_part = lax.dynamic_slice_in_dim(value_padded, first_block, group_size + 2, 0)
        key_window = jnp.concatenate([key_part[:-2], key_part[1:-1], key_part[2:]], axis=1).astype(jnp.float32)
        value_window = jnp.concatenate([value_part[:-2], value_part[1:-1], value_part[2:]], axis=1).astype(jnp.float32)
        window_scores = jnp.einsum('nqhd,nkhd->nhqk', query_part, key_window) * factor
        block_ids = first_block + jnp.arange(group_size, dtype=jnp.int32)
        key_pos = block_ids[:, None] * BLOCK - BLOCK + offsets[None, :]
        usable = (key_pos >= NG) & (key_pos < TOKENS)
        window_scores = jnp.where(usable[:, None, None, :], window_scores, -jnp.inf)
        global_scores = jnp.einsum('nqhd,khd->nhqk', query_part, global_keys) * factor
        row_top = jnp.maximum(lax.optimization_barrier(jnp.max(window_scores, axis=-1)), lax.optimization_barrier(jnp.max(global_scores, axis=-1)))[..., None]
        window_exp = jnp.exp(window_scores - row_top)
        global_exp = jnp.exp(global_scores - row_top)
        row_total = lax.optimization_barrier(jnp.sum(window_exp, axis=-1)) + lax.optimization_barrier(jnp.sum(global_exp, axis=-1))
        window_weights = lax.optimization_barrier(window_exp.astype(jnp.bfloat16)).astype(jnp.float32)
        global_weights = lax.optimization_barrier(global_exp.astype(jnp.bfloat16)).astype(jnp.float32)
        blended = jnp.einsum('nhqk,nkhd->nqhd', window_weights, value_window)
        blended = blended + jnp.einsum('nhqk,khd->nqhd', global_weights, global_values)
        blended = blended / jnp.transpose(row_total, (0, 2, 1))[..., None]
        return blended.reshape(group_size * BLOCK, D).astype(jnp.bfloat16)
    attended = lax.map(window_group, jnp.arange(blocks // group_size, dtype=jnp.int32)).reshape(TOKENS, D)
    global_queries = query_rows[:NG].reshape(NG, H, head_dim).astype(jnp.float32)
    key_all = key_rows.reshape(TOKENS // TOK_DEV, TOK_DEV, H, head_dim)
    value_all = value_rows.reshape(TOKENS // TOK_DEV, TOK_DEV, H, head_dim)

    def absorb(run_state, pieces):
        run_max, run_total, run_acc = run_state
        key_piece, value_piece = pieces
        scores = jnp.einsum('ghd,jhd->hgj', global_queries, key_piece.astype(jnp.float32), precision=lax.Precision.HIGHEST) * factor
        piece_top = lax.optimization_barrier(jnp.max(scores, axis=-1))
        piece_exp = jnp.exp(scores - piece_top[..., None])
        piece_total = lax.optimization_barrier(jnp.sum(piece_exp, axis=-1))
        piece_weights = lax.optimization_barrier(piece_exp.astype(jnp.bfloat16)).astype(jnp.float32)
        piece_acc = jnp.einsum('hgj,jhd->hgd', piece_weights, value_piece.astype(jnp.float32), precision=lax.Precision.HIGHEST)
        new_max = jnp.maximum(run_max, piece_top)
        carry_decay = jnp.exp(run_max - new_max)
        piece_decay = jnp.exp(piece_top - new_max)
        run_total = run_total * carry_decay + piece_total * piece_decay
        run_acc = run_acc * carry_decay[..., None] + piece_acc * piece_decay[..., None]
        return ((new_max, run_total, run_acc), None)
    start_state = (jnp.full((H, NG), -jnp.inf, jnp.float32), jnp.zeros((H, NG), jnp.float32), jnp.zeros((H, NG, head_dim), jnp.float32))
    final_state, unused_out = lax.scan(absorb, start_state, (key_all, value_all))
    global_out = (final_state[2] / final_state[1][..., None]).transpose(1, 0, 2).reshape(NG, D)
    attended = attended.at[:NG].set(global_out.astype(jnp.bfloat16))
    projected = jnp.dot(attended, w_out, preferred_element_type=jnp.float32)
    summed = tokens.astype(jnp.float32) + projected
    return layer_norm(summed, ln_gain, ln_bias).astype(jnp.bfloat16)
```

```python
import math

import jax
import jax.numpy as jnp
from jax import lax
from jax.experimental import pallas as pl
from jax.experimental.pallas import tpu as pltpu
from jax.sharding import PartitionSpec as P

H = 12
HD = 64
BLOCK = 64
NG = 128
HALF = 384
NT = (((1,), (1,)), ((), ()))
VM = pl.BlockSpec(memory_space=pltpu.VMEM)
SM = pl.BlockSpec(memory_space=pltpu.SMEM)


def call(body, outs, n_in, flops, moved, name, scratch=(), smem_first=False):
    specs = [VM] * n_in
    if smem_first:
        specs[0] = SM
    return pl.pallas_call(
        body,
        out_shape=outs,
        in_specs=specs,
        out_specs=jax.tree.map(lambda _: VM, outs),
        scratch_shapes=list(scratch),
        cost_estimate=pl.CostEstimate(flops=flops, bytes_accessed=moved, transcendentals=flops // 512),
        compiler_params=pltpu.CompilerParams(vmem_limit_bytes=40 * 1024 * 1024),
        name=name,
    )


def low_lanes(shape):
    return lax.broadcasted_iota(jnp.int32, shape, 1) < HD


def two_heads(rows, scale=None):
    keep = low_lanes(rows.shape)
    zero = jnp.zeros_like(rows)
    if scale is not None:
        rows = (rows.astype(jnp.float32) * scale).astype(rows.dtype)
    return jnp.concatenate([jnp.where(keep, rows, zero), jnp.where(keep, zero, rows)], axis=0)


def scores_of(queries, keys):
    return lax.dot_general(queries, keys, NT, preferred_element_type=jnp.float32)


def global_partial(gtok_ref, wq_ref, key_ref, value_ref, out_ref):
    scale = 1.0 / math.sqrt(HD)
    gq = jnp.dot(gtok_ref[...], wq_ref[...], preferred_element_type=jnp.float32).astype(jnp.bfloat16)
    lane = lax.broadcasted_iota(jnp.int32, (NG, 128), 1)
    for half in range(2):
        stats = jnp.zeros((NG, 128), jnp.float32)
        for j in range(3):
            cols = slice(half * HALF + j * 128, half * HALF + (j + 1) * 128)
            s = scores_of(two_heads(gq[:, cols], scale), key_ref[:, cols])
            top = jnp.max(s, axis=1, keepdims=True)
            e = jnp.exp(s - top)
            total = jnp.sum(e, axis=1, keepdims=True)
            acc = jnp.dot(e.astype(jnp.bfloat16), value_ref[:, cols], preferred_element_type=jnp.float32)
            out_ref[half * NG : (half + 1) * NG, j * 128 : (j + 1) * 128] = jnp.where(
                lane < HD, acc[:NG], acc[NG:]
            )
            for k in range(2):
                stats = jnp.where(lane == 2 * j + k, top[k * NG : (k + 1) * NG], stats)
                stats = jnp.where(lane == HD + 2 * j + k, total[k * NG : (k + 1) * NG], stats)
        out_ref[half * NG : (half + 1) * NG, HALF:] = stats


def merge_parts(part_ref, out_ref):
    stats = part_ref[:, HALF:]
    best = jnp.max(stats, axis=0, keepdims=True)
    weight = jnp.exp(stats - best)
    total = jnp.sum(weight * pltpu.roll(stats, HD, 1), axis=0, keepdims=True)
    n = stats.shape[0]
    keep = low_lanes((n, 128))
    keep_one = low_lanes((1, 128))
    for j in range(3):
        w = jnp.where(keep, weight[:, 2 * j : 2 * j + 1], weight[:, 2 * j + 1 : 2 * j + 2])
        t = jnp.where(keep_one, total[:, 2 * j : 2 * j + 1], total[:, 2 * j + 1 : 2 * j + 2])
        acc = jnp.sum(part_ref[:, j * 128 : (j + 1) * 128] * w, axis=0, keepdims=True)
        out_ref[:, j * 128 : (j + 1) * 128] = (acc / t).astype(jnp.bfloat16)


def window(dev_ref, last, query_ref, key_ref, value_ref, gkey_ref, gvalue_ref, out_ref, bias_ref):
    scale = 1.0 / math.sqrt(HD)
    dev = dev_ref[0]
    row = lax.broadcasted_iota(jnp.int32, (256, 256), 0)
    col = lax.broadcasted_iota(jnp.int32, (256, 256), 1)
    q_block = (row // BLOCK) % 2
    k_block = col // BLOCK
    banded = (k_block >= q_block) & (k_block <= q_block + 2)
    for m in range(2):
        position = dev * 256 + m * 128 - BLOCK + col
        usable = banded & (position >= NG) & (position < (last + 1) * 256)
        bias_ref[m] = jnp.where(usable, 0.0, -jnp.inf).astype(jnp.float32)
    keep = low_lanes((128, 128))
    for m in range(2):
        for j in range(6):
            cols = slice(j * 128, (j + 1) * 128)
            q = two_heads(query_ref[m * 128 : (m + 1) * 128, cols], scale)
            keys = slice(m * 128, m * 128 + 256)
            s_win = scores_of(q, key_ref[keys, cols]) + bias_ref[m]
            s_glob = scores_of(q, gkey_ref[:, cols])
            top = jnp.maximum(jnp.maximum(s_win[:, :128], s_win[:, 128:]), s_glob)
            top = jnp.max(top, axis=1, keepdims=True)
            e_win = jnp.exp(s_win - top)
            e_glob = jnp.exp(s_glob - top)
            total = jnp.sum(e_win[:, :128] + e_win[:, 128:] + e_glob, axis=1, keepdims=True)
            acc = jnp.dot(e_win.astype(jnp.bfloat16), value_ref[keys, cols], preferred_element_type=jnp.float32)
            acc = acc + jnp.dot(
                e_glob.astype(jnp.bfloat16), gvalue_ref[:, cols], preferred_element_type=jnp.float32
            )
            acc = acc / total
            out_ref[m * 128 : (m + 1) * 128, cols] = jnp.where(keep, acc[:128], acc[128:]).astype(jnp.bfloat16)


def finish(dev_ref, win_ref, glob_ref, tok_ref, w_ref, gain_ref, beta_ref, out_ref):
    on_first = dev_ref[0] == 0
    for m in range(2):
        rows = slice(m * 128, (m + 1) * 128)
        att = win_ref[rows]
        if m == 0:
            att = jnp.where(on_first, glob_ref[...], att)
        summed = tok_ref[rows].astype(jnp.float32) + jnp.dot(att, w_ref[...], preferred_element_type=jnp.float32)
        center = summed - jnp.mean(summed, axis=-1, keepdims=True)
        spread = jnp.mean(center * center, axis=-1, keepdims=True)
        out_ref[rows] = (center * lax.rsqrt(spread + 1e-05) * gain_ref[...] + beta_ref[...]).astype(jnp.bfloat16)


def project(inputs, weight):
    return jnp.dot(inputs, weight, preferred_element_type=jnp.float32).astype(jnp.bfloat16)


def tree_rounds(n):
    bits = [b for b in range(n.bit_length() - 2, 0, -1)] + [0]
    reached = [0]
    rounds = []
    for b in bits:
        pairs = [(i, i + (1 << b)) for i in reached]
        reached += [t for _, t in pairs]
        rounds.append((b, pairs))
    return rounds


def shards(tokens, w_query, w_key, w_value, w_out, ln_gain, ln_bias):
    bf, f32 = jnp.bfloat16, jnp.float32
    local, width = tokens.shape
    n = lax.axis_size("seq")
    dev = lax.axis_index("seq")

    with jax.named_scope("halo"):
        left = lax.ppermute(tokens[local - BLOCK :], "seq", [(i, (i + 1) % n) for i in range(n)])
        right = lax.ppermute(tokens[:BLOCK], "seq", [((i + 1) % n, i) for i in range(n)])

    with jax.named_scope("spread"):
        gtok = tokens[:NG]
        for b, pairs in tree_rounds(n):
            got = lax.ppermute(gtok, "seq", pairs)
            target = ((dev >> b) & 1) == 1
            if b == 0:
                gtok = jnp.where(target, got, gtok)
            else:
                low = dev & ((1 << b) - 1)
                gtok = jnp.where(target & (low == 0), got, gtok)

    query = project(tokens, w_query)
    key = project(tokens, w_key)
    value = project(tokens, w_value)
    part = call(
        global_partial,
        jax.ShapeDtypeStruct((2 * NG, 512), f32),
        4,
        4 * NG * 256 * 768 * 2,
        3 << 20,
        "global_partial",
    )(gtok, w_query, key, value)
    with jax.named_scope("exchange"):
        part = lax.all_to_all(part, "seq", 0, 0, tiled=True)
    row = call(merge_parts, jax.ShapeDtypeStruct((1, HALF), bf), 1, 1 << 20, 1 << 19, "merge_parts")(part)
    with jax.named_scope("collect"):
        rows = lax.all_to_all(jnp.broadcast_to(row, (n, HALF)), "seq", 0, 0, tiled=True)
    glob = jnp.concatenate([rows[:NG], rows[NG:]], axis=1)

    gkey = project(gtok, w_key)
    gvalue = project(gtok, w_value)
    halo = jnp.concatenate([left, right], axis=0)
    halo_key = project(halo, w_key)
    halo_value = project(halo, w_value)
    wide_key = jnp.concatenate([halo_key[:BLOCK], key, halo_key[BLOCK:]], axis=0)
    wide_value = jnp.concatenate([halo_value[:BLOCK], value, halo_value[BLOCK:]], axis=0)
    where = dev.reshape(1).astype(jnp.int32)

    def window_body(dev_ref, *refs):
        window(dev_ref, n - 1, *refs)

    attended = call(
        window_body,
        jax.ShapeDtypeStruct((local, width), bf),
        6,
        4 * 256 * 512 * 768 * 2,
        3 << 20,
        "window",
        scratch=[pltpu.VMEM((2, 256, 256), f32)],
        smem_first=True,
    )(where, query, wide_key, wide_value, gkey, gvalue)
    return call(
        finish,
        jax.ShapeDtypeStruct((local, width), bf),
        7,
        2 * 256 * 768 * 768,
        3 << 20,
        "finish",
        smem_first=True,
    )(where, attended, glob, tokens, w_out, ln_gain.reshape(1, -1), ln_bias.reshape(1, -1))


def solution(mesh):
    in_specs = (P("seq", None), P(), P(), P(), P(), P(), P())
    return jax.shard_map(shards, mesh=mesh, in_specs=in_specs, out_specs=P("seq", None), check_vma=False)
```

```python
import functools
import math

import jax
import jax.numpy as jnp
from jax import lax
from jax.experimental import pallas as pl
from jax.experimental.pallas import tpu as pltpu
from jax.sharding import PartitionSpec as P

H = 12
HD = 64
BLOCK = 64
NG = 128
HALF = 384
PLANE = 32
NT = (((1,), (1,)), ((), ()))
VM = pl.BlockSpec(memory_space=pltpu.VMEM)
SM = pl.BlockSpec(memory_space=pltpu.SMEM)


def call(body, outs, n_in, flops, moved, name, scratch=(), smem_first=False):
    specs = [VM] * n_in
    if smem_first:
        specs[0] = SM
    return pl.pallas_call(
        body,
        out_shape=outs,
        in_specs=specs,
        out_specs=jax.tree.map(lambda _: VM, outs),
        scratch_shapes=list(scratch),
        cost_estimate=pl.CostEstimate(flops=flops, bytes_accessed=moved, transcendentals=flops // 512),
        compiler_params=pltpu.CompilerParams(vmem_limit_bytes=40 * 1024 * 1024),
        name=name,
    )


def low_lanes(shape):
    return lax.broadcasted_iota(jnp.int32, shape, 1) < HD


def two_heads(rows, scale=None):
    keep = low_lanes(rows.shape)
    zero = jnp.zeros_like(rows)
    if scale is not None:
        rows = (rows.astype(jnp.float32) * scale).astype(rows.dtype)
    return jnp.concatenate([jnp.where(keep, rows, zero), jnp.where(keep, zero, rows)], axis=0)


def scores_of(queries, keys):
    return lax.dot_general(queries, keys, NT, preferred_element_type=jnp.float32)


def joined(piece_ref):
    return jnp.concatenate(
        [piece_ref[:16].reshape(NG, HALF), piece_ref[16:].reshape(NG, HALF)], axis=1
    )


def global_partial(piece_ref, wq_ref, key_ref, value_ref, out_ref, gtok_ref):
    scale = 1.0 / math.sqrt(HD)
    gtok_ref[...] = joined(piece_ref)
    gq = jnp.dot(gtok_ref[...], wq_ref[...], preferred_element_type=jnp.float32).astype(jnp.bfloat16)
    lane = lax.broadcasted_iota(jnp.int32, (NG, 128), 1)
    for half in range(2):
        stats = jnp.zeros((NG, 128), jnp.float32)
        for j in range(3):
            cols = slice(half * HALF + j * 128, half * HALF + (j + 1) * 128)
            s = scores_of(two_heads(gq[:, cols], scale), key_ref[:, cols])
            top = jnp.max(s, axis=1, keepdims=True)
            e = jnp.exp(s - top)
            total = jnp.sum(e, axis=1, keepdims=True)
            acc = jnp.dot(e.astype(jnp.bfloat16), value_ref[:, cols], preferred_element_type=jnp.float32)
            out_ref[half * NG : (half + 1) * NG, j * 128 : (j + 1) * 128] = jnp.where(
                lane < HD, acc[:NG], acc[NG:]
            )
            for k in range(2):
                stats = jnp.where(lane == 2 * j + k, top[k * NG : (k + 1) * NG], stats)
                stats = jnp.where(lane == HD + 2 * j + k, total[k * NG : (k + 1) * NG], stats)
        out_ref[half * NG : (half + 1) * NG, HALF:] = stats


def spread_weight(weight, j):
    keep = lax.broadcasted_iota(jnp.int32, weight.shape, weight.ndim - 1) < HD
    return jnp.where(keep, weight[..., 2 * j : 2 * j + 1], weight[..., 2 * j + 1 : 2 * j + 2])


def merge_plane(part_ref, out_ref):
    stats = part_ref[:, :, HALF:]
    best = jnp.max(stats, axis=0)
    weight = jnp.exp(stats - best[None])
    total = jnp.sum(weight * pltpu.roll(stats, HD, 2), axis=0)
    for j in range(3):
        w = spread_weight(weight, j)
        out_ref[:, j * 128 : (j + 1) * 128] = jnp.sum(part_ref[:, :, j * 128 : (j + 1) * 128] * w, axis=0)
    out_ref[:, HALF:] = jnp.where(low_lanes(best.shape), best, pltpu.roll(total, HD, 1))


def merge_column(*refs):
    part_refs, out_ref = refs[:-1], refs[-1]
    stats = [ref[:, HALF:] for ref in part_refs]
    best = functools.reduce(jnp.maximum, stats)
    weights = [jnp.exp(x - best) for x in stats]
    total = sum(w * pltpu.roll(x, HD, 1) for w, x in zip(weights, stats))
    for j in range(3):
        acc = sum(
            ref[:, j * 128 : (j + 1) * 128] * spread_weight(w, j) for ref, w in zip(part_refs, weights)
        )
        out_ref[:, j * 128 : (j + 1) * 128] = (acc / spread_weight(total, j)).astype(jnp.bfloat16)


def window(dev_ref, last, query_ref, key_ref, value_ref, gkey_ref, gvalue_ref, out_ref, bias_ref):
    scale = 1.0 / math.sqrt(HD)
    dev = dev_ref[0]
    row = lax.broadcasted_iota(jnp.int32, (256, 256), 0)
    col = lax.broadcasted_iota(jnp.int32, (256, 256), 1)
    q_block = (row // BLOCK) % 2
    k_block = col // BLOCK
    banded = (k_block >= q_block) & (k_block <= q_block + 2)
    for m in range(2):
        position = dev * 256 + m * 128 - BLOCK + col
        usable = banded & (position >= NG) & (position < (last + 1) * 256)
        bias_ref[m] = jnp.where(usable, 0.0, -jnp.inf).astype(jnp.float32)
    keep = low_lanes((128, 128))
    for m in range(2):
        for j in range(6):
            cols = slice(j * 128, (j + 1) * 128)
            q = two_heads(query_ref[m * 128 : (m + 1) * 128, cols], scale)
            keys = slice(m * 128, m * 128 + 256)
            s_win = scores_of(q, key_ref[keys, cols]) + bias_ref[m]
            s_glob = scores_of(q, gkey_ref[:, cols])
            top = jnp.maximum(jnp.maximum(s_win[:, :128], s_win[:, 128:]), s_glob)
            top = jnp.max(top, axis=1, keepdims=True)
            e_win = jnp.exp(s_win - top)
            e_glob = jnp.exp(s_glob - top)
            total = jnp.sum(e_win[:, :128] + e_win[:, 128:] + e_glob, axis=1, keepdims=True)
            acc = jnp.dot(e_win.astype(jnp.bfloat16), value_ref[keys, cols], preferred_element_type=jnp.float32)
            acc = acc + jnp.dot(
                e_glob.astype(jnp.bfloat16), gvalue_ref[:, cols], preferred_element_type=jnp.float32
            )
            acc = acc / total
            out_ref[m * 128 : (m + 1) * 128, cols] = jnp.where(keep, acc[:128], acc[128:]).astype(jnp.bfloat16)


def finish(dev_ref, win_ref, glob_ref, tok_ref, w_ref, gain_ref, beta_ref, out_ref):
    on_first = dev_ref[0] == 0
    for m in range(2):
        rows = slice(m * 128, (m + 1) * 128)
        att = win_ref[rows]
        if m == 0:
            att = jnp.where(on_first, joined(glob_ref), att)
        summed = tok_ref[rows].astype(jnp.float32) + jnp.dot(att, w_ref[...], preferred_element_type=jnp.float32)
        center = summed - jnp.mean(summed, axis=-1, keepdims=True)
        spread = jnp.mean(center * center, axis=-1, keepdims=True)
        out_ref[rows] = (center * lax.rsqrt(spread + 1e-05) * gain_ref[...] + beta_ref[...]).astype(jnp.bfloat16)


def project(inputs, weight):
    return jnp.dot(inputs, weight, preferred_element_type=jnp.float32).astype(jnp.bfloat16)


def shards(tokens, w_query, w_key, w_value, w_out, ln_gain, ln_bias):
    bf, f32 = jnp.bfloat16, jnp.float32
    local, width = tokens.shape
    n = lax.axis_size("seq")
    dev = lax.axis_index("seq")

    with jax.named_scope("halo"):
        left = lax.ppermute(tokens[local - BLOCK :], "seq", [(i, (i + 1) % n) for i in range(n)])
        right = lax.ppermute(tokens[:BLOCK], "seq", [((i + 1) % n, i) for i in range(n)])

    planes = n // PLANE
    groups = [[z * PLANE + r for r in range(PLANE)] for z in range(planes)]
    z = dev // PLANE

    def exchange(chunks):
        return lax.all_to_all(chunks, "seq", 0, 0, tiled=True, axis_index_groups=groups)

    def along_z(x, pairs):
        return lax.ppermute(x, "seq", [(a * PLANE + r, b * PLANE + r) for a, b in pairs for r in range(PLANE)])

    def pieces_of(rows):
        return jnp.concatenate([rows[:, :HALF].reshape(16, 8, HALF), rows[:, HALF:].reshape(16, 8, HALF)], axis=0)

    with jax.named_scope("scatter"):
        piece = exchange(pieces_of(tokens[:NG]))[0]
    with jax.named_scope("spread"):
        up = along_z(piece, [(0, 3)])
        down = along_z(piece, [(0, 5)])
        piece = jnp.where(z == 3, up, jnp.where(z == 5, down, piece))
        up = along_z(piece, [(0, 1), (3, 4), (5, 6)])
        down = along_z(piece, [(0, 7), (3, 2)])
        piece = jnp.where((z == 1) | (z == 4) | (z == 6), up, jnp.where((z == 7) | (z == 2), down, piece))
    with jax.named_scope("gather"):
        pieces = exchange(jnp.broadcast_to(piece[None], (PLANE, 8, HALF)))

    query = project(tokens, w_query)
    key = project(tokens, w_key)
    value = project(tokens, w_value)
    part, gtok = call(
        global_partial,
        (jax.ShapeDtypeStruct((2 * NG, 512), f32), jax.ShapeDtypeStruct((NG, width), bf)),
        4,
        4 * NG * 256 * 768 * 2,
        3 << 20,
        "global_partial",
    )(pieces, w_query, key, value)
    with jax.named_scope("parts"):
        part = exchange(part.reshape(PLANE, 8, 512))
    part = call(merge_plane, jax.ShapeDtypeStruct((8, 512), f32), 1, 1 << 20, 1 << 19, "merge_plane")(part)
    with jax.named_scope("column"):
        others = [along_z(part, [(k, 0)]) for k in (4, 3, 5, 2, 6, 1, 7)]
    row = call(merge_column, jax.ShapeDtypeStruct((8, HALF), bf), 8, 1 << 18, 1 << 17, "merge_column")(part, *others)
    with jax.named_scope("collect"):
        glob = exchange(jnp.broadcast_to(row[None], (PLANE, 8, HALF)))

    gkey = project(gtok, w_key)
    gvalue = project(gtok, w_value)
    halo = jnp.concatenate([left, right], axis=0)
    halo_key = project(halo, w_key)
    halo_value = project(halo, w_value)
    wide_key = jnp.concatenate([halo_key[:BLOCK], key, halo_key[BLOCK:]], axis=0)
    wide_value = jnp.concatenate([halo_value[:BLOCK], value, halo_value[BLOCK:]], axis=0)
    where = dev.reshape(1).astype(jnp.int32)

    def window_body(dev_ref, *refs):
        window(dev_ref, n - 1, *refs)

    attended = call(
        window_body,
        jax.ShapeDtypeStruct((local, width), bf),
        6,
        4 * 256 * 512 * 768 * 2,
        3 << 20,
        "window",
        scratch=[pltpu.VMEM((2, 256, 256), f32)],
        smem_first=True,
    )(where, query, wide_key, wide_value, gkey, gvalue)
    return call(
        finish,
        jax.ShapeDtypeStruct((local, width), bf),
        7,
        2 * 256 * 768 * 768,
        3 << 20,
        "finish",
        smem_first=True,
    )(where, attended, glob, tokens, w_out, ln_gain.reshape(1, -1), ln_bias.reshape(1, -1))


def solution(mesh):
    in_specs = (P("seq", None), P(), P(), P(), P(), P(), P())
    return jax.shard_map(shards, mesh=mesh, in_specs=in_specs, out_specs=P("seq", None), check_vma=False)
```

```python
import functools
import math

import jax
import jax.numpy as jnp
from jax import lax
from jax.experimental import pallas as pl
from jax.experimental.pallas import tpu as pltpu
from jax.sharding import PartitionSpec as P

H = 12
HD = 64
BLOCK = 64
NG = 128
HALF = 384
PLANE = 32
NT = (((1,), (1,)), ((), ()))
VM = pl.BlockSpec(memory_space=pltpu.VMEM)
SM = pl.BlockSpec(memory_space=pltpu.SMEM)
HB = pl.BlockSpec(memory_space=pl.ANY)
DMA = pltpu.SemaphoreType.DMA
WEIGHT = pltpu.VMEM((768, 768), jnp.bfloat16)


def call(body, outs, specs, flops, moved, name, scratch=(), aliases=None, out_spec=VM, mib=60):
    return pl.pallas_call(
        body,
        out_shape=outs,
        in_specs=list(specs),
        out_specs=jax.tree.map(lambda _: out_spec, outs),
        scratch_shapes=list(scratch),
        input_output_aliases=aliases or {},
        cost_estimate=pl.CostEstimate(flops=flops, bytes_accessed=moved, transcendentals=flops // 512),
        compiler_params=pltpu.CompilerParams(vmem_limit_bytes=mib * 1024 * 1024),
        name=name,
    )


def loads(sem, pairs):
    copies = [pltpu.make_async_copy(src, dst, sem.at[i]) for i, (src, dst) in enumerate(pairs)]
    for copy in copies:
        copy.start()
    return copies


def dot(a, b):
    return jnp.dot(a, b, preferred_element_type=jnp.float32)


def low_lanes(shape):
    return lax.broadcasted_iota(jnp.int32, shape, 1) < HD


def two_heads(rows, scale=None):
    keep = low_lanes(rows.shape)
    zero = jnp.zeros_like(rows)
    if scale is not None:
        rows = (rows.astype(jnp.float32) * scale).astype(rows.dtype)
    return jnp.concatenate([jnp.where(keep, rows, zero), jnp.where(keep, zero, rows)], axis=0)


def scores_of(queries, keys):
    return lax.dot_general(queries, keys, NT, preferred_element_type=jnp.float32)


def joined(piece_ref):
    return jnp.concatenate(
        [piece_ref[:16].reshape(NG, HALF), piece_ref[16:].reshape(NG, HALF)], axis=1
    )


def chosen(dev_ref, on_plane_0):
    plane_0 = dev_ref[0] < PLANE
    return plane_0 if on_plane_0 else jnp.logical_not(plane_0)


def own_rows(on_plane_0, dev_ref, tok_hbm, wq_hbm, wk_hbm, wv_hbm, *refs):
    outs = refs[-10:-7]
    tok, wq, wk, wv, res, sem, out_sem = refs[-7:]

    @pl.when(chosen(dev_ref, on_plane_0))
    def _():
        copies = loads(sem, [(tok_hbm, tok), (wk_hbm, wk), (wv_hbm, wv), (wq_hbm, wq)])
        copies[0].wait()
        sent = []
        for i, w in enumerate((wk, wv, wq)):
            copies[1 + i].wait()
            res[i] = dot(tok[...], w[...]).astype(jnp.bfloat16)
            copy = pltpu.make_async_copy(res.at[i], outs[i], out_sem.at[i])
            copy.start()
            sent.append(copy)
        for copy in sent:
            copy.wait()


def global_partial(piece_hbm, wq_hbm, key_hbm, value_hbm, out_ref, pieces, wq, key, value, sem):
    copies = loads(sem, [(piece_hbm, pieces), (wq_hbm, wq), (key_hbm, key), (value_hbm, value)])
    scale = 1.0 / math.sqrt(HD)
    copies[0].wait()
    copies[1].wait()
    gq = dot(joined(pieces), wq[...]).astype(jnp.bfloat16)
    copies[2].wait()
    copies[3].wait()
    lane = lax.broadcasted_iota(jnp.int32, (NG, 128), 1)
    for half in range(2):
        rows = slice(half * NG, (half + 1) * NG)
        stats = jnp.zeros((NG, 128), jnp.float32)
        for j in range(3):
            cols = slice(half * HALF + j * 128, half * HALF + (j + 1) * 128)
            s = scores_of(two_heads(gq[:, cols], scale), key[:, cols])
            top = jnp.max(s, axis=1, keepdims=True)
            e = jnp.exp(s - top)
            total = jnp.sum(e, axis=1, keepdims=True)
            acc = dot(e.astype(jnp.bfloat16), value[:, cols])
            out_ref[rows, j * 128 : (j + 1) * 128] = jnp.where(lane < HD, acc[:NG], acc[NG:]).astype(jnp.bfloat16)
            for k in range(2):
                pick = (lane % 16 == 2 * j + k) & (lane < 48)
                stats = jnp.where(pick, top[k * NG : (k + 1) * NG], stats)
                pick = (lane % 16 == 8 + 2 * j + k) & (lane < 48)
                stats = jnp.where(pick, total[k * NG : (k + 1) * NG], stats)
        high = stats.astype(jnp.bfloat16)
        rest = stats - high.astype(jnp.float32)
        mid = rest.astype(jnp.bfloat16)
        low = (rest - mid.astype(jnp.float32)).astype(jnp.bfloat16)
        packed = jnp.where(
            lane < 16,
            high.astype(jnp.float32),
            jnp.where(lane < 32, mid.astype(jnp.float32), low.astype(jnp.float32)),
        )
        out_ref[rows, HALF:] = packed.astype(jnp.bfloat16)


def spread_weight(weight, j):
    keep = lax.broadcasted_iota(jnp.int32, weight.shape, weight.ndim - 1) < HD
    return jnp.where(keep, weight[..., 2 * j : 2 * j + 1], weight[..., 2 * j + 1 : 2 * j + 2])


def merge_plane(part_ref, out_ref):
    packed = part_ref[:, :, HALF:].astype(jnp.float32)
    stats = (packed + pltpu.roll(packed, 112, 2)) + pltpu.roll(packed, 96, 2)
    best = jnp.max(stats, axis=0)
    weight = jnp.exp(stats - best[None])
    total = jnp.sum(weight * pltpu.roll(stats, 120, 2), axis=0)
    for j in range(3):
        w = spread_weight(weight, j)
        acc = part_ref[:, :, j * 128 : (j + 1) * 128].astype(jnp.float32) * w
        out_ref[:, j * 128 : (j + 1) * 128] = jnp.sum(acc, axis=0)
    out_ref[:, HALF:] = jnp.where(low_lanes(best.shape), best, pltpu.roll(total, HD, 1))


def merged_parts(part_refs):
    stats = [ref[:, HALF:] for ref in part_refs]
    tops = [jnp.where(pltpu.roll(x, HD, 1) > 0, x, -jnp.inf) for x in stats]
    best = functools.reduce(jnp.maximum, tops)
    weights = [jnp.exp(x - best) for x in tops]
    total = sum(w * pltpu.roll(x, HD, 1) for w, x in zip(weights, stats))
    accs = [
        sum(ref[:, j * 128 : (j + 1) * 128] * spread_weight(w, j) for ref, w in zip(part_refs, weights))
        for j in range(3)
    ]
    return best, total, accs


def merge_hop(*refs):
    best, total, accs = merged_parts(refs[:-1])
    for j in range(3):
        refs[-1][:, j * 128 : (j + 1) * 128] = accs[j]
    refs[-1][:, HALF:] = jnp.where(low_lanes(best.shape), best, pltpu.roll(total, HD, 1))


def merge_column(*refs):
    _, total, accs = merged_parts(refs[:-1])
    for j in range(3):
        refs[-1][:, j * 128 : (j + 1) * 128] = (accs[j] / spread_weight(total, j)).astype(jnp.bfloat16)


def window(last, dev_ref, *refs):
    window_rows(dev_ref[0], last, *refs)


def window_rows(
    dev, last, after_hbm, tok_hbm, left_hbm, right_hbm, piece_hbm, wk_hbm, wv_hbm, wo_hbm, query_hbm, key_hbm, value_hbm,
    gain_ref, beta_ref, *refs,
):
    out_hbm, pieces, wk, wv, wo, tok, halo, query, key, value, gkey, gvalue, att, res, bias_ref, sem = refs[-16:]
    own = slice(BLOCK, BLOCK + 256)
    copies = loads(
        sem,
        [
            (piece_hbm, pieces),
            (wk_hbm, wk),
            (left_hbm, halo.at[:BLOCK]),
            (right_hbm, halo.at[BLOCK:]),
            (wv_hbm, wv),
            (query_hbm, query),
            (key_hbm, key.at[own]),
            (value_hbm, value.at[own]),
            (tok_hbm, tok),
            (wo_hbm, wo),
        ],
    )
    scale = 1.0 / math.sqrt(HD)
    row = lax.broadcasted_iota(jnp.int32, (256, 256), 0)
    col = lax.broadcasted_iota(jnp.int32, (256, 256), 1)
    q_block = (row // BLOCK) % 2
    k_block = col // BLOCK
    banded = (k_block >= q_block) & (k_block <= q_block + 2)
    for m in range(2):
        position = dev * 256 + m * 128 - BLOCK + col
        usable = banded & (position >= NG) & (position < (last + 1) * 256)
        bias_ref[m] = jnp.where(usable, 0.0, -jnp.inf).astype(jnp.float32)
    for copy in copies[:4]:
        copy.wait()
    gtok = joined(pieces)
    both = jnp.concatenate([gtok, halo[...]], axis=0)
    for w, copy, glob, wide in ((wk, None, gkey, key), (wv, copies[4], gvalue, value)):
        if copy is not None:
            copy.wait()
        made = dot(both, w[...]).astype(jnp.bfloat16)
        glob[...] = made[:NG]
        wide[:BLOCK] = made[NG : NG + BLOCK]
        wide[BLOCK + 256 :] = made[NG + BLOCK :]
    for copy in copies[5:8]:
        copy.wait()
    keep = low_lanes((128, 128))
    for m in range(2):
        for j in range(6):
            cols = slice(j * 128, (j + 1) * 128)
            q = two_heads(query[m * 128 : (m + 1) * 128, cols], scale)
            keys = slice(m * 128, m * 128 + 256)
            s_win = scores_of(q, key[keys, cols]) + bias_ref[m]
            s_glob = scores_of(q, gkey[:, cols])
            top = jnp.maximum(jnp.maximum(s_win[:, :128], s_win[:, 128:]), s_glob)
            top = jnp.max(top, axis=1, keepdims=True)
            e_win = jnp.exp(s_win - top)
            e_glob = jnp.exp(s_glob - top)
            total = jnp.sum(e_win[:, :128] + e_win[:, 128:] + e_glob, axis=1, keepdims=True)
            acc = dot(e_win.astype(jnp.bfloat16), value[keys, cols])
            acc = acc + dot(e_glob.astype(jnp.bfloat16), gvalue[:, cols])
            acc = acc / total
            att[m * 128 : (m + 1) * 128, cols] = jnp.where(keep, acc[:128], acc[128:]).astype(jnp.bfloat16)
    for copy in copies[8:]:
        copy.wait()
    for m in range(2):
        rows = slice(m * 128, (m + 1) * 128)
        res[rows] = encode(att[rows], tok[rows], wo[...], gain_ref[...], beta_ref[...])
    copy = pltpu.make_async_copy(res, out_hbm, sem.at[10])
    copy.start()
    copy.wait()


def encode(att, tok, w, gain, beta):
    summed = tok.astype(jnp.float32) + dot(att, w)
    center = summed - jnp.mean(summed, axis=-1, keepdims=True)
    spread = jnp.mean(center * center, axis=-1, keepdims=True)
    return (center * lax.rsqrt(spread + 1e-05) * gain + beta).astype(jnp.bfloat16)


def finish_first(
    dev_ref, glob_hbm, tok_hbm, w_hbm, gain_ref, beta_ref, done_hbm, out_hbm, glob, tok, w, res, sem
):
    @pl.when(dev_ref[0] == 0)
    def _():
        for copy in loads(sem, [(glob_hbm, glob), (tok_hbm.at[:NG], tok), (w_hbm, w)]):
            copy.wait()
        res[...] = encode(joined(glob), tok[...], w[...], gain_ref[...], beta_ref[...])
        copy = pltpu.make_async_copy(res, out_hbm.at[:NG], sem.at[3])
        copy.start()
        copy.wait()


def shards(tokens, w_query, w_key, w_value, w_out, ln_gain, ln_bias):
    bf, f32 = jnp.bfloat16, jnp.float32
    local, width = tokens.shape
    n = lax.axis_size("seq")
    dev = lax.axis_index("seq")
    where = dev.reshape(1).astype(jnp.int32)
    gain, beta = ln_gain.reshape(1, -1), ln_bias.reshape(1, -1)

    planes = n // PLANE
    groups = [[z * PLANE + r for r in range(PLANE)] for z in range(planes)]
    z = lax.shift_right_logical(dev, 5)

    def exchange(chunks):
        return lax.all_to_all(chunks, "seq", 0, 0, tiled=True, axis_index_groups=groups)

    def along_z(x, pairs):
        return lax.ppermute(x, "seq", [(a * PLANE + r, b * PLANE + r) for a, b in pairs for r in range(PLANE)])

    shape = jax.ShapeDtypeStruct
    rows = shape((local, width), bf)
    tok_scratch = pltpu.VMEM((local, width), bf)
    piece_scratch = pltpu.VMEM((PLANE, 8, HALF), bf)
    half_scratch = pltpu.VMEM((NG, width), bf)
    wide_scratch = pltpu.VMEM((local + 2 * BLOCK, width), bf)

    def own(on_plane_0, earlier, after):
        return call(
            functools.partial(own_rows, on_plane_0), (rows,) * 3, [SM] + [HB] * (5 + len(earlier)),
            6 * 256 * 768 * 768, 4 << 20, "own_rows",
            scratch=[tok_scratch, WEIGHT, WEIGHT, WEIGHT, pltpu.VMEM((3, local, width), bf), DMA((4,)), DMA((3,))],
            aliases={5 + i: i for i in range(len(earlier))}, out_spec=HB,
        )(where, tokens, w_query, w_key, w_value, *earlier, after)

    chunks = tokens[:NG].reshape(16, 8, 2, HALF).transpose(2, 0, 1, 3).reshape(PLANE, 8, HALF)
    with jax.named_scope("scatter"):
        piece = exchange(chunks)[0]
    with jax.named_scope("spread"):
        up = along_z(piece, [(0, 3)])
        down = along_z(piece, [(0, 5)])
        made = own(False, (), piece)
        piece = jnp.where(z == 3, up, jnp.where(z == 5, down, piece))
        piece, made = lax.optimization_barrier((piece, made))
        up = along_z(piece, [(0, 1), (3, 4), (5, 6)])
        down = along_z(piece, [(0, 7), (3, 2)])
        made = own(True, made, piece)
        piece = jnp.where((z == 1) | (z == 4) | (z == 6), up, jnp.where((z == 7) | (z == 2), down, piece))
    piece, made = lax.optimization_barrier((piece, made))
    key, value, query = made
    spread = jnp.broadcast_to(piece[None], (PLANE, 8, HALF))
    with jax.named_scope("gather"):
        pieces = exchange(spread)
    with jax.named_scope("halo"):
        edges, _ = lax.optimization_barrier((tokens, spread))
        left = lax.ppermute(edges[local - BLOCK :], "seq", [(i, (i + 1) % n) for i in range(n)])
        right = lax.ppermute(edges[:BLOCK], "seq", [((i + 1) % n, i) for i in range(n)])

    part = call(
        global_partial, shape((2 * NG, 512), bf), [HB] * 4, 4 * NG * 256 * 768 * 2, 3 << 20, "global_partial",
        scratch=[piece_scratch, WEIGHT, tok_scratch, tok_scratch, DMA((4,))],
    )(pieces, w_query, key, value)
    with jax.named_scope("parts"):
        merged = exchange(part.reshape(PLANE, 8, 512))

    def windowed(after):
        return call(
            functools.partial(window, n - 1), rows,
            [SM] + [HB] * 11 + [VM] * 2, 4 * 256 * 512 * 768 * 2, 4 << 20, "window",
            scratch=[
                piece_scratch, WEIGHT, WEIGHT, WEIGHT, tok_scratch, half_scratch, tok_scratch, wide_scratch,
                wide_scratch, half_scratch, half_scratch, tok_scratch, tok_scratch,
                pltpu.VMEM((2, 256, 256), f32), DMA((11,)),
            ],
            out_spec=HB,
        )(
            where, after, tokens, left, right, pieces, w_key, w_value, w_out, query, key, value, gain, beta
        )

    merged, left, right = lax.optimization_barrier((merged, left, right))
    merged = call(merge_plane, shape((8, 512), f32), [VM], 1 << 20, 1 << 19, "merge_plane", mib=8)(merged)
    with jax.named_scope("column"):
        up = along_z(merged, [(7, 0), (2, 3)])
        down = along_z(merged, [(1, 0), (4, 3), (6, 5)])
        merged = call(merge_hop, shape((8, 512), f32), [VM] * 3, 1 << 18, 1 << 17, "merge_hop", mib=8)(merged, up, down)
        others = [along_z(merged, [(5, 0)]), along_z(merged, [(3, 0)])]
    row = call(merge_column, shape((8, HALF), bf), [VM] * 3, 1 << 18, 1 << 17, "merge_column", mib=8)(merged, *others)
    with jax.named_scope("collect"):
        glob = exchange(jnp.broadcast_to(row[None], (PLANE, 8, HALF)))
    done = windowed(row)
    glob, done = lax.optimization_barrier((glob, done))
    return call(
        finish_first, rows, [SM] + [HB] * 3 + [VM] * 2 + [HB], 2 * 128 * 768 * 768, 3 << 20, "finish_first",
        scratch=[piece_scratch, half_scratch, WEIGHT, half_scratch, DMA((4,))],
        aliases={6: 0}, out_spec=HB,
    )(where, glob, tokens, w_out, gain, beta, done)


def solution(mesh):
    in_specs = (P("seq", None), P(), P(), P(), P(), P(), P())
    return jax.shard_map(shards, mesh=mesh, in_specs=in_specs, out_specs=P("seq", None), check_vma=False)
```

```python
import functools
import math

import jax
import jax.numpy as jnp
from jax import lax
from jax.experimental import pallas as pl
from jax.experimental.pallas import tpu as pltpu
from jax.sharding import PartitionSpec as P

H = 12
HD = 64
BLOCK = 64
NG = 128
HALF = 384
PLANE = 32
NT = (((1,), (1,)), ((), ()))
VM = pl.BlockSpec(memory_space=pltpu.VMEM)
SM = pl.BlockSpec(memory_space=pltpu.SMEM)
HB = pl.BlockSpec(memory_space=pl.ANY)
DMA = pltpu.SemaphoreType.DMA
WEIGHT = pltpu.VMEM((768, 768), jnp.bfloat16)


def call(body, outs, specs, flops, moved, name, scratch=(), aliases=None, out_spec=VM, mib=60):
    return pl.pallas_call(
        body,
        out_shape=outs,
        in_specs=list(specs),
        out_specs=jax.tree.map(lambda _: out_spec, outs),
        scratch_shapes=list(scratch),
        input_output_aliases=aliases or {},
        cost_estimate=pl.CostEstimate(flops=flops, bytes_accessed=moved, transcendentals=flops // 512),
        compiler_params=pltpu.CompilerParams(vmem_limit_bytes=mib * 1024 * 1024),
        name=name,
    )


def loads(sem, pairs):
    copies = [pltpu.make_async_copy(src, dst, sem.at[i]) for i, (src, dst) in enumerate(pairs)]
    for copy in copies:
        copy.start()
    return copies


def dot(a, b):
    return jnp.dot(a, b, preferred_element_type=jnp.float32)


def low_lanes(shape):
    return lax.broadcasted_iota(jnp.int32, shape, 1) < HD


def two_heads(rows, scale=None):
    keep = low_lanes(rows.shape)
    zero = jnp.zeros_like(rows)
    if scale is not None:
        rows = (rows.astype(jnp.float32) * scale).astype(rows.dtype)
    return jnp.concatenate([jnp.where(keep, rows, zero), jnp.where(keep, zero, rows)], axis=0)


def scores_of(queries, keys):
    return lax.dot_general(queries, keys, NT, preferred_element_type=jnp.float32)


def joined(piece_ref):
    return jnp.concatenate(
        [piece_ref[:16].reshape(NG, HALF), piece_ref[16:].reshape(NG, HALF)], axis=1
    )


def chosen(dev_ref, on_plane_0):
    plane_0 = dev_ref[0] < PLANE
    return plane_0 if on_plane_0 else jnp.logical_not(plane_0)


def own_rows(on_plane_0, dev_ref, tok_hbm, wq_hbm, wk_hbm, wv_hbm, *refs):
    outs = refs[-10:-7]
    tok, wq, wk, wv, res, sem, out_sem = refs[-7:]

    @pl.when(chosen(dev_ref, on_plane_0))
    def _():
        copies = loads(sem, [(tok_hbm, tok), (wk_hbm, wk), (wv_hbm, wv), (wq_hbm, wq)])
        copies[0].wait()
        sent = []
        for i, w in enumerate((wk, wv, wq)):
            copies[1 + i].wait()
            res[i] = dot(tok[...], w[...]).astype(jnp.bfloat16)
            copy = pltpu.make_async_copy(res.at[i], outs[i], out_sem.at[i])
            copy.start()
            sent.append(copy)
        for copy in sent:
            copy.wait()


def global_partial(piece_hbm, wq_hbm, key_hbm, value_hbm, out_ref, pieces, wq, key, value, sem):
    copies = loads(sem, [(piece_hbm, pieces), (wq_hbm, wq), (key_hbm, key), (value_hbm, value)])
    scale = 1.0 / math.sqrt(HD)
    copies[0].wait()
    copies[1].wait()
    gq = dot(joined(pieces), wq[...]).astype(jnp.bfloat16)
    copies[2].wait()
    copies[3].wait()
    lane = lax.broadcasted_iota(jnp.int32, (NG, 128), 1)
    for half in range(2):
        rows = slice(half * NG, (half + 1) * NG)
        stats = jnp.zeros((NG, 128), jnp.float32)
        for j in range(3):
            cols = slice(half * HALF + j * 128, half * HALF + (j + 1) * 128)
            s = scores_of(two_heads(gq[:, cols], scale), key[:, cols])
            top = jnp.max(s, axis=1, keepdims=True)
            e = jnp.exp(s - top)
            total = jnp.sum(e, axis=1, keepdims=True)
            acc = dot(e.astype(jnp.bfloat16), value[:, cols])
            out_ref[rows, j * 128 : (j + 1) * 128] = jnp.where(lane < HD, acc[:NG], acc[NG:]).astype(jnp.bfloat16)
            for k in range(2):
                pick = (lane % 16 == 2 * j + k) & (lane < 48)
                stats = jnp.where(pick, top[k * NG : (k + 1) * NG], stats)
                pick = (lane % 16 == 8 + 2 * j + k) & (lane < 48)
                stats = jnp.where(pick, total[k * NG : (k + 1) * NG], stats)
        high = stats.astype(jnp.bfloat16)
        rest = stats - high.astype(jnp.float32)
        mid = rest.astype(jnp.bfloat16)
        low = (rest - mid.astype(jnp.float32)).astype(jnp.bfloat16)
        packed = jnp.where(
            lane < 16,
            high.astype(jnp.float32),
            jnp.where(lane < 32, mid.astype(jnp.float32), low.astype(jnp.float32)),
        )
        out_ref[rows, HALF:] = packed.astype(jnp.bfloat16)


def spread_weight(weight, j):
    keep = lax.broadcasted_iota(jnp.int32, weight.shape, weight.ndim - 1) < HD
    return jnp.where(keep, weight[..., 2 * j : 2 * j + 1], weight[..., 2 * j + 1 : 2 * j + 2])


def merge_plane(part_ref, out_ref):
    packed = part_ref[:, :, HALF:].astype(jnp.float32)
    stats = (packed + pltpu.roll(packed, 112, 2)) + pltpu.roll(packed, 96, 2)
    best = jnp.max(stats, axis=0)
    weight = jnp.exp(stats - best[None])
    total = jnp.sum(weight * pltpu.roll(stats, 120, 2), axis=0)
    for j in range(3):
        w = spread_weight(weight, j)
        acc = part_ref[:, :, j * 128 : (j + 1) * 128].astype(jnp.float32) * w
        out_ref[:, j * 128 : (j + 1) * 128] = jnp.sum(acc, axis=0)
    out_ref[:, HALF:] = jnp.where(low_lanes(best.shape), best, pltpu.roll(total, HD, 1))


def merged_parts(part_refs):
    stats = [ref[:, HALF:] for ref in part_refs]
    tops = [jnp.where(pltpu.roll(x, HD, 1) > 0, x, -jnp.inf) for x in stats]
    best = functools.reduce(jnp.maximum, tops)
    weights = [jnp.exp(x - best) for x in tops]
    total = sum(w * pltpu.roll(x, HD, 1) for w, x in zip(weights, stats))
    accs = [
        sum(ref[:, j * 128 : (j + 1) * 128] * spread_weight(w, j) for ref, w in zip(part_refs, weights))
        for j in range(3)
    ]
    return best, total, accs


def merge_hop(*refs):
    best, total, accs = merged_parts(refs[:-1])
    for j in range(3):
        refs[-1][:, j * 128 : (j + 1) * 128] = accs[j]
    refs[-1][:, HALF:] = jnp.where(low_lanes(best.shape), best, pltpu.roll(total, HD, 1))


def merge_column(*refs):
    _, total, accs = merged_parts(refs[:-1])
    for j in range(3):
        refs[-1][:, j * 128 : (j + 1) * 128] = (accs[j] / spread_weight(total, j)).astype(jnp.bfloat16)


def window(last, dev_ref, *refs):
    window_rows(dev_ref[0], last, *refs)


def window_rows(
    dev, last, after_hbm, tok_hbm, left_hbm, right_hbm, piece_hbm, wk_hbm, wv_hbm, wo_hbm, query_hbm, key_hbm, value_hbm,
    gain_ref, beta_ref, *refs,
):
    out_hbm, pieces, wk, wv, wo, tok, halo, query, key, value, gkey, gvalue, att, res, bias_ref, sem = refs[-16:]
    own = slice(BLOCK, BLOCK + 256)
    copies = loads(
        sem,
        [
            (piece_hbm, pieces),
            (wk_hbm, wk),
            (left_hbm, halo.at[:BLOCK]),
            (right_hbm, halo.at[BLOCK:]),
            (wv_hbm, wv),
            (query_hbm, query),
            (key_hbm, key.at[own]),
            (value_hbm, value.at[own]),
            (tok_hbm, tok),
            (wo_hbm, wo),
        ],
    )
    scale = 1.0 / math.sqrt(HD)
    row = lax.broadcasted_iota(jnp.int32, (256, 256), 0)
    col = lax.broadcasted_iota(jnp.int32, (256, 256), 1)
    q_block = (row // BLOCK) % 2
    k_block = col // BLOCK
    banded = (k_block >= q_block) & (k_block <= q_block + 2)
    for m in range(2):
        position = dev * 256 + m * 128 - BLOCK + col
        usable = banded & (position >= NG) & (position < (last + 1) * 256)
        bias_ref[m] = jnp.where(usable, 0.0, -jnp.inf).astype(jnp.float32)
    for copy in copies[:4]:
        copy.wait()
    gtok = joined(pieces)
    both = jnp.concatenate([gtok, halo[...]], axis=0)
    for w, copy, glob, wide in ((wk, None, gkey, key), (wv, copies[4], gvalue, value)):
        if copy is not None:
            copy.wait()
        made = dot(both, w[...]).astype(jnp.bfloat16)
        glob[...] = made[:NG]
        wide[:BLOCK] = made[NG : NG + BLOCK]
        wide[BLOCK + 256 :] = made[NG + BLOCK :]
    for copy in copies[5:8]:
        copy.wait()
    keep = low_lanes((128, 128))
    for m in range(2):
        for j in range(6):
            cols = slice(j * 128, (j + 1) * 128)
            q = two_heads(query[m * 128 : (m + 1) * 128, cols], scale)
            keys = slice(m * 128, m * 128 + 256)
            s_win = scores_of(q, key[keys, cols]) + bias_ref[m]
            s_glob = scores_of(q, gkey[:, cols])
            top = jnp.maximum(jnp.maximum(s_win[:, :128], s_win[:, 128:]), s_glob)
            top = jnp.max(top, axis=1, keepdims=True)
            e_win = jnp.exp(s_win - top)
            e_glob = jnp.exp(s_glob - top)
            total = jnp.sum(e_win[:, :128] + e_win[:, 128:] + e_glob, axis=1, keepdims=True)
            acc = dot(e_win.astype(jnp.bfloat16), value[keys, cols])
            acc = acc + dot(e_glob.astype(jnp.bfloat16), gvalue[:, cols])
            acc = acc / total
            att[m * 128 : (m + 1) * 128, cols] = jnp.where(keep, acc[:128], acc[128:]).astype(jnp.bfloat16)
    for copy in copies[8:]:
        copy.wait()
    for m in range(2):
        rows = slice(m * 128, (m + 1) * 128)
        res[rows] = encode(att[rows], tok[rows], wo[...], gain_ref[...], beta_ref[...])
    copy = pltpu.make_async_copy(res, out_hbm, sem.at[10])
    copy.start()
    copy.wait()


def encode(att, tok, w, gain, beta):
    summed = tok.astype(jnp.float32) + dot(att, w)
    center = summed - jnp.mean(summed, axis=-1, keepdims=True)
    spread = jnp.mean(center * center, axis=-1, keepdims=True)
    return (center * lax.rsqrt(spread + 1e-05) * gain + beta).astype(jnp.bfloat16)


def finish_first(
    dev_ref, glob, tok_hbm, w_hbm, gain_ref, beta_ref, done_hbm, out_hbm, tok, w, res, sem
):
    @pl.when(dev_ref[0] == 0)
    def _():
        for copy in loads(sem, [(w_hbm, w), (tok_hbm.at[:NG], tok)]):
            copy.wait()
        res[...] = encode(joined(glob), tok[...], w[...], gain_ref[...], beta_ref[...])
        copy = pltpu.make_async_copy(res, out_hbm.at[:NG], sem.at[2])
        copy.start()
        copy.wait()


def shards(tokens, w_query, w_key, w_value, w_out, ln_gain, ln_bias):
    bf, f32 = jnp.bfloat16, jnp.float32
    local, width = tokens.shape
    n = lax.axis_size("seq")
    dev = lax.axis_index("seq")
    where = dev.reshape(1).astype(jnp.int32)
    gain, beta = ln_gain.reshape(1, -1), ln_bias.reshape(1, -1)

    planes = n // PLANE
    groups = [[z * PLANE + r for r in range(PLANE)] for z in range(planes)]
    z = lax.shift_right_logical(dev, 5)

    def exchange(chunks):
        return lax.all_to_all(chunks, "seq", 0, 0, tiled=True, axis_index_groups=groups)

    def along_z(x, pairs):
        return lax.ppermute(x, "seq", [(a * PLANE + r, b * PLANE + r) for a, b in pairs for r in range(PLANE)])

    shape = jax.ShapeDtypeStruct
    rows = shape((local, width), bf)
    tok_scratch = pltpu.VMEM((local, width), bf)
    piece_scratch = pltpu.VMEM((PLANE, 8, HALF), bf)
    half_scratch = pltpu.VMEM((NG, width), bf)
    wide_scratch = pltpu.VMEM((local + 2 * BLOCK, width), bf)

    def own(on_plane_0, earlier, after):
        return call(
            functools.partial(own_rows, on_plane_0), (rows,) * 3, [SM] + [HB] * (5 + len(earlier)),
            6 * 256 * 768 * 768, 4 << 20, "own_rows",
            scratch=[tok_scratch, WEIGHT, WEIGHT, WEIGHT, pltpu.VMEM((3, local, width), bf), DMA((4,)), DMA((3,))],
            aliases={5 + i: i for i in range(len(earlier))}, out_spec=HB,
        )(where, tokens, w_query, w_key, w_value, *earlier, after)

    chunks = tokens[:NG].reshape(16, 8, 2, HALF).transpose(2, 0, 1, 3).reshape(PLANE, 8, HALF)
    with jax.named_scope("scatter"):
        piece, gain, beta = lax.optimization_barrier((exchange(chunks), gain, beta))
        piece = piece[0]
    with jax.named_scope("spread"):
        up = along_z(piece, [(0, 3)])
        down = along_z(piece, [(0, 5)])
        made = own(False, (), piece)
        piece = jnp.where(z == 3, up, jnp.where(z == 5, down, piece))
        piece, made = lax.optimization_barrier((piece, made))
        up = along_z(piece, [(0, 1), (3, 4), (5, 6)])
        down = along_z(piece, [(0, 7), (3, 2)])
        made = own(True, made, piece)
        piece = jnp.where((z == 1) | (z == 4) | (z == 6), up, jnp.where((z == 7) | (z == 2), down, piece))
    piece, made = lax.optimization_barrier((piece, made))
    key, value, query = made
    spread = jnp.broadcast_to(piece[None], (PLANE, 8, HALF))
    with jax.named_scope("gather"):
        pieces = exchange(spread)
    with jax.named_scope("halo"):
        edges, _ = lax.optimization_barrier((tokens, spread))
        left = lax.ppermute(edges[local - BLOCK :], "seq", [(i, (i + 1) % n) for i in range(n)])
        right = lax.ppermute(edges[:BLOCK], "seq", [((i + 1) % n, i) for i in range(n)])

    part = call(
        global_partial, shape((2 * NG, 512), bf), [HB] * 4, 4 * NG * 256 * 768 * 2, 3 << 20, "global_partial",
        scratch=[piece_scratch, WEIGHT, tok_scratch, tok_scratch, DMA((4,))],
    )(pieces, w_query, key, value)
    with jax.named_scope("parts"):
        merged = exchange(part.reshape(PLANE, 8, 512))

    def windowed(after):
        return call(
            functools.partial(window, n - 1), rows,
            [SM] + [HB] * 11 + [VM] * 2, 4 * 256 * 512 * 768 * 2, 4 << 20, "window",
            scratch=[
                piece_scratch, WEIGHT, WEIGHT, WEIGHT, tok_scratch, half_scratch, tok_scratch, wide_scratch,
                wide_scratch, half_scratch, half_scratch, tok_scratch, tok_scratch,
                pltpu.VMEM((2, 256, 256), f32), DMA((11,)),
            ],
            out_spec=HB,
        )(
            where, after, tokens, left, right, pieces, w_key, w_value, w_out, query, key, value, gain, beta
        )

    merged, left, right = lax.optimization_barrier((merged, left, right))
    merged = call(merge_plane, shape((8, 512), f32), [VM], 1 << 20, 1 << 19, "merge_plane", mib=8)(merged)
    with jax.named_scope("column"):
        up = along_z(merged, [(7, 0), (2, 3)])
        down = along_z(merged, [(1, 0), (4, 3), (6, 5)])
        merged = call(merge_hop, shape((8, 512), f32), [VM] * 3, 1 << 18, 1 << 17, "merge_hop", mib=8)(merged, up, down)
        others = [along_z(merged, [(5, 0)]), along_z(merged, [(3, 0)])]
    row = call(merge_column, shape((8, HALF), bf), [VM] * 3, 1 << 18, 1 << 17, "merge_column", mib=8)(merged, *others)
    with jax.named_scope("collect"):
        glob = exchange(jnp.broadcast_to(row[None], (PLANE, 8, HALF)))
    done = windowed(row)
    glob, done = lax.optimization_barrier((glob, done))
    return call(
        finish_first, rows, [SM, VM] + [HB] * 2 + [VM] * 2 + [HB], 2 * 128 * 768 * 768, 3 << 20, "finish_first",
        scratch=[half_scratch, WEIGHT, half_scratch, DMA((3,))],
        aliases={6: 0}, out_spec=HB,
    )(where, glob, tokens, w_out, gain, beta, done)


def solution(mesh):
    in_specs = (P("seq", None), P(), P(), P(), P(), P(), P())
    return jax.shard_map(shards, mesh=mesh, in_specs=in_specs, out_specs=P("seq", None), check_vma=False)
```
